32 devices in a mesh: groups: 2 (over y), vox: 4 (over z), chan: 2 (over x), frm: 2 (over core).
Axes of the slice: x: 2, y: 2, z: 4, core: 2. Of those that a mesh axis runs over, the one named last changes fastest.
Arguments:
- echo_data: bfloat16 [8, 2, 1024, 2, 512], P(('groups', 'vox'), 'chan', None, None, 'frm'), parts along dimension 0, may hold values from -36 to 36
- tile_weights: bfloat16 [4, 2, 64, 128, 128], P('vox', 'chan'), may hold values from -0.0625 to 0.0625
- tile_target: int32 [4, 2, 64], P('vox', 'chan'), may hold values from 0 to 1
- tile_offset: int32 [4, 2, 64], P('vox', 'chan'), may hold values from 0 to 896
- tile_count: int32 [4, 2], P('vox', 'chan'), may hold values from 8 to 64, as said below
- grid_map: int32 [4, 256], P('vox'), may hold values from 0 to 255, each once within a row
- psf_kernel: float32 [5, 5], replicated, may hold values from -1.25 to 1.25
Outputs:
- psf_image: float32 [64, 32, 512], P(('groups', 'vox'), 'chan', 'frm'), parts along dimension 0
The draws below stay inside these ranges and needn't reach their ends.
There are 2 independent parts, one for each index of `groups`. The reference program is written for one: setup_inputs(seed, part) draws one part's arguments, and reference() takes and returns one part's arrays. A program takes and returns all parts, laid end to end along the dimension named above; an argument that names none is the same for every part. Nothing has to cross between parts.
Inputs may be any that keep to these rules, and one draw needn't show every extreme that they name: `tile_count`: in each voxel block exactly one channel group uses all 64 slots; the others use far fewer. `grid_map`: each block's row is a permutation of 0 to 255.
All inputs are finite; a program needn't handle non-finite values.
Results may differ from the reference program's by a relative error of at most 0.014.
Values may be sent and summed in bfloat16 or wider, within the bound.
A program may use at most 64 MiB of HBM per device.

```python
import math
import jax
import jax.numpy as jnp
from jax import lax

FRAMES = 512
TILE = 128
VOX_DEV = 256
ROWS = 1024
TCAP = 64
BLOCKS = 4
CGROUPS = 2
NA = 32
NB = 32


def draw_echo_data(key, part):
    key_rows, key_frames, key_values = jax.random.split(jax.random.fold_in(key, 5), 3)
    shape_all = (BLOCKS, CGROUPS, ROWS, 2, FRAMES)
    row_scale = jnp.exp(jax.random.uniform(key_rows, (BLOCKS, CGROUPS, ROWS, 1, 1), jnp.float32, math.log(0.3), math.log(3.0)))
    frame_scale = jnp.exp(jax.random.uniform(key_frames, (FRAMES,), jnp.float32, 0.0, math.log(3.0)))
    values = jax.random.truncated_normal(key_values, -4.0, 4.0, shape_all, jnp.float32)
    return (values * row_scale * frame_scale).astype(jnp.bfloat16)


def draw_tile_count(key, part):
    key_busy, key_base = jax.random.split(jax.random.fold_in(key, 11))
    busiest = jax.random.randint(key_busy, (BLOCKS, 1), 0, CGROUPS)
    base_counts = jax.random.randint(key_base, (BLOCKS, CGROUPS), TCAP // 8, TCAP // 3 + 1)
    group_ids = jnp.arange(CGROUPS, dtype=jnp.int32)[None, :]
    return jnp.where(group_ids == busiest, TCAP, base_counts).astype(jnp.int32)


def plant(entries, key, least, high):
    extent = entries.shape
    spot = [jax.random.randint(jax.random.fold_in(key, axis), (), 0, extent[axis]) for axis in range(len(extent))]
    entries = entries.at[tuple(spot)].set(least)
    longest = extent.index(max(extent))
    spot[longest] = (spot[longest] + 1) % extent[longest]
    return entries.at[tuple(spot)].set(high)


def block_scale(stream_key, extent, cuts, least, largest):
    level, own = 1.0, jax.random.fold_in(stream_key, 6)
    for dim, parts in cuts:
        steps = jnp.exp(jax.random.uniform(jax.random.fold_in(own, dim), (parts,), jnp.float32, least / len(cuts), largest / len(cuts)))
        level = level * jnp.repeat(steps, extent[dim] // parts).reshape([-1 if axis == dim else 1 for axis in range(len(extent))])
    return level


def scatter_about(rng, dims, deviation, most, cuts=(), kind=jnp.bfloat16):
    result = deviation * jax.random.normal(rng, dims, jnp.float32)
    if cuts:
        result = result * block_scale(rng, dims, cuts, -0.22, 0.18)
    return jnp.clip(result, -most, most).astype(kind)


def setup_inputs(seed: int = 0, part: int = 0) -> dict:
    key_of = jax.random.split(jax.random.key(seed), 8)
    part_keys = jax.random.split(jax.random.fold_in(key_of[7], part), 8)
    return {
        "echo_data": draw_echo_data(jax.random.fold_in(jax.random.fold_in(key_of[7], part), 71), part),
        "tile_weights": scatter_about(key_of[1], (BLOCKS, CGROUPS, TCAP, TILE, TILE), (TILE * TCAP) ** -0.5, 0.0625, ((0, 4), (1, 2))),
        "tile_target": plant(jax.random.randint(key_of[2], (BLOCKS, CGROUPS, TCAP), 0, VOX_DEV // TILE), jax.random.fold_in(key_of[2], 1), 0, (VOX_DEV // TILE) - 1).astype(jnp.int32),
        "tile_offset": plant(jax.random.randint(key_of[3], (BLOCKS, CGROUPS, TCAP), 0, ROWS - TILE + 1), jax.random.fold_in(key_of[3], 1), 0, ROWS - TILE).astype(jnp.int32),
        "tile_count": draw_tile_count(jax.random.fold_in(key_of[7], 71), part),
        "grid_map": jax.vmap(lambda own: jax.random.permutation(own, VOX_DEV))(jax.random.split(key_of[5], BLOCKS)).reshape((BLOCKS, VOX_DEV)).astype(jnp.int32),
        "psf_kernel": scatter_about(key_of[6], (5, 5), 25 ** -0.5, 1.25, (), jnp.float32),
    }


POLY_COEFFS = (1.0, -0.6, 0.15, -0.03)

def complex_times(left_real, left_imag, right_real, right_imag):
    level = lax.Precision.HIGH
    real_part = jnp.dot(left_real, right_real, precision=level, preferred_element_type=jnp.float32) - jnp.dot(left_imag, right_imag, precision=level, preferred_element_type=jnp.float32)
    imag_part = jnp.dot(left_real, right_imag, precision=level, preferred_element_type=jnp.float32) + jnp.dot(left_imag, right_real, precision=level, preferred_element_type=jnp.float32)
    return (real_part, imag_part)

def beam_block(block_items):
    echo_block, weight_block, target_block, offset_block, count_block = block_items
    group_total = echo_block.shape[0]
    flat_echo = echo_block.reshape(group_total, ROWS, 2 * FRAMES)
    slot_total = group_total * TCAP
    slot_ids = jnp.arange(slot_total, dtype=jnp.int32)
    group_ids = slot_ids // TCAP
    keep_slots = slot_ids % TCAP < count_block[group_ids]
    zero_index = jnp.zeros((), jnp.int32)

    def add_tile(totals, item):
        weight_tile, group_id, target_id, offset_id, keep_tile = item
        samples = lax.dynamic_slice(flat_echo, (group_id, offset_id, zero_index), (1, TILE, 2 * FRAMES))[0]
        product = jnp.dot(weight_tile, samples, preferred_element_type=jnp.float32)
        product = jnp.where(keep_tile, product, jnp.zeros_like(product))
        return (totals.at[target_id].add(product), None)
    start_totals = jnp.zeros((VOX_DEV // TILE, TILE, 2 * FRAMES), jnp.float32)
    items = (weight_block.reshape(slot_total, TILE, TILE), group_ids, target_block.reshape(slot_total), offset_block.reshape(slot_total), keep_slots)
    totals, unused = lax.scan(add_tile, start_totals, items)
    return totals.reshape(VOX_DEV, 2, FRAMES)

def reference(echo_data, tile_weights, tile_target, tile_offset, tile_count, grid_map, psf_kernel):
    beams = lax.map(beam_block, (echo_data, tile_weights, tile_target, tile_offset, tile_count))
    arranged = jax.vmap(lambda beam_rows, order_ids: beam_rows[order_ids])(beams, grid_map)
    beamformed = arranged.reshape(NA, NB, 2, FRAMES).astype(jnp.bfloat16)
    stacked = beamformed.reshape(NA * NB, 2 * FRAMES)
    gram_block = lax.dot_general(stacked, stacked, (((0,), (0,)), ((), ())), preferred_element_type=jnp.float32)
    gram_real = gram_block[:FRAMES, :FRAMES] + gram_block[FRAMES:, FRAMES:]
    gram_imag = gram_block[:FRAMES, FRAMES:] - gram_block[FRAMES:, :FRAMES]
    factor = FRAMES / jnp.trace(gram_real)
    norm_real = factor * gram_real
    norm_imag = factor * gram_imag
    echo_real = beamformed[:, :, 0, :].reshape(NA * NB, FRAMES).astype(jnp.float32)
    echo_imag = beamformed[:, :, 1, :].reshape(NA * NB, FRAMES).astype(jnp.float32)
    term_real = POLY_COEFFS[3] * echo_real
    term_imag = POLY_COEFFS[3] * echo_imag
    for degree in (2, 1, 0):
        term_real, term_imag = complex_times(term_real, term_imag, norm_real, norm_imag)
        term_real = term_real + POLY_COEFFS[degree] * echo_real
        term_imag = term_imag + POLY_COEFFS[degree] * echo_imag
    envelope = jnp.sqrt(term_real * term_real + term_imag * term_imag + 1e-06)
    envelope = envelope.reshape(NA, NB, FRAMES)
    padded = jnp.pad(envelope, ((2, 2), (2, 2), (0, 0)))
    psf_image = jnp.zeros_like(envelope)
    for shift_a in range(5):
        for shift_b in range(5):
            psf_image = psf_image + psf_kernel[shift_a, shift_b] * padded[shift_a:shift_a + NA, shift_b:shift_b + NB]
    return psf_image
```

```python
import functools

import jax
import jax.numpy as jnp
from jax import lax
from jax.experimental import pallas as pl
from jax.experimental.pallas import tpu as pltpu
from jax.sharding import PartitionSpec as P

MESH = pl.DeviceIdType.MESH

TBATCH = 8
LAT_DEV = 8


POLY_COEFFS = (1.0, -0.6, 0.15, -0.03)


def with_halo(shard, sides, width):
    for axis, dim in sides:
        devices, length = (lax.axis_size(axis), shard.shape[dim])
        up = [(i, (i + 1) % devices) for i in range(devices - 1)]
        down = [(j, i) for i, j in up]
        last = lax.slice_in_dim(shard, length - width, length, axis=dim)
        leading = lax.slice_in_dim(shard, 0, width, axis=dim)
        before = lax.ppermute(last, axis, up)
        after = lax.ppermute(leading, axis, down)
        shard = jnp.concatenate([before, shard, after], axis=dim)
    return shard


def complex_times(left_real, left_imag, right_real, right_imag):
    level = lax.Precision.HIGH
    real_part = jnp.dot(
        left_real, right_real, precision=level, preferred_element_type=jnp.float32
    ) - jnp.dot(left_imag, right_imag, precision=level, preferred_element_type=jnp.float32)
    imag_part = jnp.dot(
        left_real, right_imag, precision=level, preferred_element_type=jnp.float32
    ) + jnp.dot(left_imag, right_real, precision=level, preferred_element_type=jnp.float32)
    return (real_part, imag_part)


def tile_pass(flat_echo, weights, tile_goal, tile_start, live_total, tiles_out):
    tile_size = weights.shape[-1]
    col_count = flat_echo.shape[-1]
    slot_count = weights.shape[0]
    lane_ids = jnp.arange(TBATCH, dtype=jnp.int32)
    target_ids = jnp.arange(tiles_out, dtype=jnp.int32)
    zero_index = jnp.zeros((), jnp.int32)

    def cut_rows(offset_id):
        return lax.dynamic_slice(flat_echo, (offset_id, zero_index), (tile_size, col_count))

    def one_turn(turn_index, totals):
        where_at = turn_index * TBATCH + lane_ids
        live_lane = where_at < live_total
        chosen = jnp.minimum(where_at, slot_count - 1)
        picked = weights[chosen]
        samples = jax.vmap(cut_rows)(tile_start[chosen])
        product = jnp.einsum("krs,ksc->krc", picked, samples, preferred_element_type=jnp.float32)
        placing = ((tile_goal[chosen][:, None] == target_ids[None, :]) & live_lane[:, None]).astype(
            jnp.float32
        )
        return totals + jnp.einsum(
            "kt,krc->trc", placing, product, precision=lax.Precision.HIGHEST
        )

    start_totals = jnp.zeros((tiles_out, tile_size, col_count), jnp.float32)
    turn_count = (live_total + TBATCH - 1) // TBATCH
    return lax.fori_loop(0, turn_count, one_turn, start_totals)


def shards(echo_data, tile_weights, tile_target, tile_offset, tile_count, grid_map, psf_kernel):
    row_count = echo_data.shape[2]
    half_frames = echo_data.shape[4]
    tile_size = tile_weights.shape[-1]
    slot_count = tile_weights.shape[2]
    voxels = grid_map.shape[1]
    tiles_out = voxels // tile_size
    flat_echo = echo_data.reshape(row_count, 2 * half_frames)
    weights = tile_weights.reshape(slot_count, tile_size, tile_size)
    tile_sums = tile_pass(
        flat_echo,
        weights,
        tile_target.reshape(-1),
        tile_offset.reshape(-1),
        tile_count[0, 0],
        tiles_out,
    )
    arranged = jnp.take(tile_sums.reshape(voxels, 2, half_frames), grid_map[0], axis=0)
    arranged = arranged.reshape(LAT_DEV, voxels // LAT_DEV, 2, half_frames)
    beamformed = lax.psum_scatter(arranged, "chan", scatter_dimension=1, tiled=True).astype(
        jnp.bfloat16
    )
    lat_count = beamformed.shape[0]
    depth_count = beamformed.shape[1]
    cell_count = lat_count * depth_count
    own_frames = beamformed.reshape(cell_count, 2, half_frames)
    all_frames = lax.all_gather(own_frames, "frm", axis=2, tiled=True)
    frames = all_frames.shape[2]
    own_flat = own_frames.reshape(cell_count, 2 * half_frames)
    all_flat = all_frames.reshape(cell_count, 2 * frames)
    gram_block = lax.dot_general(
        own_flat, all_flat, (((0,), (0,)), ((), ())), preferred_element_type=jnp.float32
    )
    gram_real = gram_block[:half_frames, :frames] + gram_block[half_frames:, frames:]
    gram_imag = gram_block[:half_frames, frames:] - gram_block[half_frames:, :frames]
    frame_start = lax.axis_index("frm") * half_frames
    echo_real = all_frames[:, 0, :].astype(jnp.float32)
    echo_imag = all_frames[:, 1, :].astype(jnp.float32)
    energy = jnp.sum(echo_real * echo_real + echo_imag * echo_imag)
    gram_real, gram_imag, trace_value = lax.psum((gram_real, gram_imag, energy), ("vox", "chan"))
    factor = frames / trace_value
    norm_real = factor * gram_real
    norm_imag = factor * gram_imag
    full_real, full_imag = (
        lax.all_gather(norm_real, "frm", axis=0, tiled=True),
        lax.all_gather(norm_imag, "frm", axis=0, tiled=True),
    )
    identity = jnp.eye(frames, dtype=jnp.float32)
    poly_real = POLY_COEFFS[3] * full_real + POLY_COEFFS[2] * identity
    poly_imag = POLY_COEFFS[3] * full_imag
    poly_real, poly_imag = complex_times(poly_real, poly_imag, full_real, full_imag)
    poly_real = poly_real + POLY_COEFFS[1] * identity
    cols_real = lax.dynamic_slice_in_dim(full_real, frame_start, half_frames, 1)
    cols_imag = lax.dynamic_slice_in_dim(full_imag, frame_start, half_frames, 1)
    filter_real, filter_imag = complex_times(poly_real, poly_imag, cols_real, cols_imag)
    filter_real = filter_real + POLY_COEFFS[0] * lax.dynamic_slice_in_dim(
        identity, frame_start, half_frames, 1
    )
    out_real, out_imag = complex_times(echo_real, echo_imag, filter_real, filter_imag)
    envelope = jnp.sqrt(out_real * out_real + out_imag * out_imag + 1e-06)
    envelope = envelope.reshape(lat_count, depth_count, half_frames)
    padded = with_halo(envelope, (("vox", 0), ("chan", 1)), 2)
    psf_image = jnp.zeros_like(envelope)
    for shift_a in range(5):
        for shift_b in range(5):
            psf_image = (
                psf_image
                + psf_kernel[shift_a, shift_b]
                * padded[shift_a : shift_a + lat_count, shift_b : shift_b + depth_count]
            )
    return psf_image


def split(value):
    high = value.astype(jnp.bfloat16)
    return high, (value - high.astype(jnp.float32)).astype(jnp.bfloat16)


def beam_kernel(goal_ref, start_ref, live_ref, weights_ref, echo_ref, map_ref, out_ref, operator, high_ref, low_ref):
    blocks, voxels, tile = operator.shape
    operator[...] = jnp.zeros_like(operator)
    lane = lax.broadcasted_iota(jnp.int32, (tile, tile), 1)

    def place(slot, carry):
        first = start_ref[slot]
        block = first // tile
        shift = first - block * tile
        rows = pl.ds(pl.multiple_of(goal_ref[slot] * tile, tile), tile)
        turned = pltpu.roll(weights_ref[slot].astype(jnp.float32), shift, 1)
        operator[block, rows, :] += jnp.where(lane >= shift, turned, 0.0)
        operator[block + 1, rows, :] += jnp.where(lane < shift, turned, 0.0)
        return carry

    lax.fori_loop(0, live_ref[0], place, 0)
    picks = lax.broadcasted_iota(jnp.int32, (voxels, voxels), 0) == map_ref[...]
    picks = picks.astype(jnp.float32).T.astype(jnp.bfloat16)
    for block in range(blocks - 1):
        high, low = split(operator[block])
        columns = slice(block * tile, (block + 1) * tile)
        for part, target in ((high, high_ref), (low, low_ref)):
            moved = jnp.dot(picks, part, preferred_element_type=jnp.float32)
            target[:, columns] = moved.astype(jnp.bfloat16)
    sums = jnp.dot(high_ref[...], echo_ref[...], preferred_element_type=jnp.float32)
    sums += jnp.dot(low_ref[...], echo_ref[...], preferred_element_type=jnp.float32)
    halves, cells, _ = out_ref.shape
    width = cells // LAT_DEV
    for lat in range(LAT_DEV):
        for half in range(halves):
            source = (lat * halves + half) * width
            out_ref[half, lat * width : (lat + 1) * width, :] = sums[source : source + width]


def gather_kernel(
    count, part_ref, out_ref, arrived, once_send, once_recv, own_recv, mate_recv, up_send, down_send, mate_send
):
    vox, chan, frm = lax.axis_index("vox"), lax.axis_index("chan"), lax.axis_index("frm")
    beside, mate = {"chan": 1 - chan}, {"frm": 1 - frm}
    above, below = {"vox": vox + 1}, {"vox": vox - 1}
    can_up, can_down = vox + 1 < count, vox > 0
    barrier = pltpu.get_barrier_semaphore()

    def greet(target):
        pl.semaphore_signal(barrier, inc=1, device_id=target, device_id_type=MESH)

    greet(beside)
    greet(mate)
    pl.when(can_up)(lambda: greet(above))
    pl.when(can_down)(lambda: greet(below))
    pl.semaphore_wait(barrier, 4 - jnp.where(can_up, 0, 1) - jnp.where(can_down, 0, 1))

    def remote(source, target, sent, received, device):
        return pltpu.make_async_remote_copy(
            src_ref=source, dst_ref=target, send_sem=sent, recv_sem=received, device_id=device, device_id_type=MESH
        )

    def item(block, side, sent, device):
        place = out_ref.at[block, side, frm]
        return remote(place, place, sent, own_recv.at[block, side], device)

    def to_mate(block, side):
        place = out_ref.at[block, side, frm]
        return remote(place, place, mate_send.at[block, side], mate_recv.at[block, side], mate)

    def go_up(block, side):
        return item(block, side, up_send.at[block, side], above)

    def go_down(block, side):
        return item(block, side, down_send.at[block, side], below)

    def landed(block, side):
        item(block, side, once_send.at[1], beside).wait_recv()

    swap = remote(part_ref.at[1 - chan], arrived, once_send.at[0], once_recv.at[0], beside)
    swap.start()
    swap.wait()
    out_ref[vox, chan, frm] = (part_ref[chan] + arrived[...]).astype(out_ref.dtype)
    across = item(vox, chan, once_send.at[1], beside)
    across.start()

    def spread(side):
        pl.when(can_up)(lambda: go_up(vox, side).start())
        pl.when(can_down)(lambda: go_down(vox, side).start())
        to_mate(vox, side).start()

    spread(chan)
    landed(vox, 1 - chan)
    spread(1 - chan)
    for step in range(1, count):
        for turn in range(2):
            side = chan if turn == 0 else 1 - chan

            @pl.when(vox >= step)
            def _():
                landed(vox - step, side)
                pl.when(can_up)(lambda: go_up(vox - step, side).start())
                to_mate(vox - step, side).start()

            @pl.when(vox + step < count)
            def _():
                landed(vox + step, side)
                pl.when(can_down)(lambda: go_down(vox + step, side).start())
                to_mate(vox + step, side).start()

    across.wait_send()
    for block in range(count):
        for side in range(2):
            copy = to_mate(block, side)
            copy.wait_send()
            place = out_ref.at[block, side, 1 - frm]
            remote(place, place, mate_send.at[block, side], mate_recv.at[block, side], mate).wait_recv()
            pl.when(can_up & (vox >= block))(lambda: go_up(block, side).wait_send())
            pl.when(can_down & (vox <= block))(lambda: go_down(block, side).wait_send())


def filter_kernel(count, beams_ref, psf_ref, out_ref, high_ref, low_ref, padded):
    vox, chan, frm = lax.axis_index("vox"), lax.axis_index("chan"), lax.axis_index("frm")
    lat, depth, half = out_ref.shape
    cells = lat * depth
    pair = 2 * half
    total = count * 2 * cells
    left = beams_ref[:, :, 0].reshape(total, pair)
    right = beams_ref[:, :, 1].reshape(total, pair)

    def gram(first, second):
        block = lax.dot_general(first, second, (((0,), (0,)), ((), ())), preferred_element_type=jnp.float32)
        real = block[:half, :half] + block[half:, half:]
        imag = block[:half, half:] - block[half:, :half]
        return real, imag

    grams = {(0, 0): gram(left, left), (0, 1): gram(left, right), (1, 1): gram(right, right)}
    grams[1, 0] = (grams[0, 1][0].T, -grams[0, 1][1].T)
    eye = lax.broadcasted_iota(jnp.int32, (half, half), 0) == lax.broadcasted_iota(jnp.int32, (half, half), 1)
    diagonal = jnp.where(eye, grams[0, 0][0] + grams[1, 1][0], 0.0)
    trace = jnp.sum(jnp.sum(diagonal, axis=0, keepdims=True), axis=1, keepdims=True)
    factor = (2 * half) / trace
    for (row, column), (real, imag) in grams.items():
        real_parts, imag_parts = split(factor * real), split(factor * imag)
        for target, real_part, imag_part in zip((high_ref, low_ref), real_parts, imag_parts):
            top, side = row * pair, column * pair
            target[top : top + half, side : side + half] = real_part
            target[top : top + half, side + half : side + pair] = imag_part
            target[top + half : top + pair, side : side + half] = -imag_part
            target[top + half : top + pair, side + half : side + pair] = real_part

    before, after = jnp.maximum(vox - 1, 0), jnp.minimum(vox + 1, count - 1)
    edge = 2 * depth

    def both(block, side, rows):
        return jnp.concatenate([beams_ref[block, side, 0, rows], beams_ref[block, side, 1, rows]], axis=1)

    other = 1 - chan
    near = jnp.concatenate(
        [
            both(before, other, slice(cells - edge, cells)),
            both(vox, other, slice(0, cells)),
            both(after, other, slice(0, edge)),
        ],
        axis=0,
    )
    tall = lat + 4
    slots = -(-2 * tall // 16) * 16
    picked = lax.broadcasted_iota(jnp.int32, (slots, tall * depth), 0)
    source = lax.broadcasted_iota(jnp.int32, (slots, tall * depth), 1)
    wanted = (picked // 2) * depth + picked % 2 + jnp.where(chan == 0, 0, depth - 2)
    picks = ((source == wanted) & (picked < 2 * tall)).astype(jnp.float32).astype(jnp.bfloat16)
    near = jnp.dot(picks, near, preferred_element_type=jnp.float32).astype(jnp.bfloat16)
    beams = jnp.concatenate(
        [
            both(before, chan, slice(cells - edge, cells)),
            both(vox, chan, slice(0, cells)),
            both(after, chan, slice(0, edge)),
            near,
        ],
        axis=0,
    )

    def times(high, low, columns):
        result = jnp.dot(high, high_ref[:, columns], preferred_element_type=jnp.float32)
        result += jnp.dot(high, low_ref[:, columns], preferred_element_type=jnp.float32)
        if low is not None:
            result += jnp.dot(low, high_ref[:, columns], preferred_element_type=jnp.float32)
        return result

    echo = beams.astype(jnp.float32)
    whole = slice(0, 2 * pair)
    term = POLY_COEFFS[3] * times(beams, None, whole) + POLY_COEFFS[2] * echo
    term = times(*split(term), whole) + POLY_COEFFS[1] * echo
    own = pl.ds(pl.multiple_of(frm * pair, pair), pair)
    echo = jnp.where(frm == 0, echo[:, :pair], echo[:, pair:])
    term = times(*split(term), own) + POLY_COEFFS[0] * echo
    envelope = jnp.sqrt(term[:, :half] * term[:, :half] + term[:, half:] * term[:, half:] + 1e-06)

    padded[...] = jnp.zeros_like(padded)
    has_before, has_after = jnp.where(vox > 0, 1.0, 0.0), jnp.where(vox + 1 < count, 1.0, 0.0)
    right_side, left_side = jnp.where(chan == 0, 1.0, 0.0), jnp.where(chan == 0, 0.0, 1.0)
    for line in range(tall):
        scale = has_before if line < 2 else has_after if line >= lat + 2 else None
        middle = envelope[line * depth : (line + 1) * depth]
        start = tall * depth + 2 * line
        rim = envelope[start : start + 2]
        if scale is not None:
            middle, rim = middle * scale, rim * scale
        padded[line, 8 : 8 + depth, :] = middle
        padded[line, 6:8, :] = rim * left_side
        padded[line, 8 + depth : 10 + depth, :] = rim * right_side
    result = jnp.zeros((lat, depth, half), jnp.float32)
    for shift_b in range(5):
        for shift_a in range(5):
            result += psf_ref[shift_a, shift_b] * padded[shift_a : shift_a + lat, 6 + shift_b : 6 + shift_b + depth]
    out_ref[...] = result


def kernel_shards(count, echo_data, tile_weights, tile_target, tile_offset, tile_count, grid_map, psf_kernel):
    rows, half = echo_data.shape[2], echo_data.shape[4]
    slots, tile = tile_weights.shape[2], tile_weights.shape[4]
    voxels = grid_map.shape[1]
    cells, pair = voxels // 2, 2 * half
    depth = cells // LAT_DEV
    vmem, smem = pl.BlockSpec(memory_space=pltpu.VMEM), pl.BlockSpec(memory_space=pltpu.SMEM)
    parts = pl.pallas_call(
        beam_kernel,
        name="beam",
        out_shape=jax.ShapeDtypeStruct((2, cells, pair), jnp.float32),
        in_specs=[smem, smem, smem, vmem, vmem, vmem],
        out_specs=vmem,
        scratch_shapes=[
            pltpu.VMEM((rows // tile + 1, voxels, tile), jnp.float32),
            pltpu.VMEM((voxels, rows), jnp.bfloat16),
            pltpu.VMEM((voxels, rows), jnp.bfloat16),
        ],
    )(
        tile_target.reshape(-1),
        tile_offset.reshape(-1),
        tile_count.reshape(-1),
        tile_weights.reshape(slots, tile, tile),
        echo_data.reshape(rows, pair),
        grid_map,
    )
    pairs = (count, 2)
    dma = pltpu.SemaphoreType.DMA
    beams = pl.pallas_call(
        functools.partial(gather_kernel, count),
        name="gather",
        out_shape=jax.ShapeDtypeStruct((count, 2, 2, cells, pair), jnp.bfloat16),
        in_specs=[vmem],
        out_specs=vmem,
        scratch_shapes=[pltpu.VMEM((cells, pair), jnp.float32), dma((2,)), dma((1,))] + [dma(pairs)] * 5,
        compiler_params=pltpu.CompilerParams(collective_id=0, has_side_effects=True),
    )(parts)
    return pl.pallas_call(
        functools.partial(filter_kernel, count),
        name="filter",
        out_shape=jax.ShapeDtypeStruct((LAT_DEV, depth, half), jnp.float32),
        in_specs=[vmem, smem],
        out_specs=vmem,
        scratch_shapes=[
            pltpu.VMEM((2 * pair, 2 * pair), jnp.bfloat16),
            pltpu.VMEM((2 * pair, 2 * pair), jnp.bfloat16),
            pltpu.VMEM((LAT_DEV + 4, depth + 16, half), jnp.float32),
        ],
    )(beams, psf_kernel)


def solution(mesh):
    in_specs = (
        P(("groups", "vox"), "chan", None, None, "frm"),
        P("vox", "chan", None, None, None),
        P("vox", "chan", None),
        P("vox", "chan", None),
        P("vox", "chan"),
        P("vox", None),
        P(),
    )
    out_specs = P(("groups", "vox"), "chan", "frm")
    body = shards
    if mesh.shape["chan"] == 2 and mesh.shape["frm"] == 2:
        body = functools.partial(kernel_shards, mesh.shape["vox"])
    return jax.shard_map(body, mesh=mesh, in_specs=in_specs, out_specs=out_specs, check_vma=False)
```

```python
import functools

import jax
import jax.numpy as jnp
from jax import lax
from jax.experimental import pallas as pl
from jax.experimental.pallas import tpu as pltpu
from jax.sharding import PartitionSpec as P

MESH = pl.DeviceIdType.MESH
PIECES = 4
GROUP = 8

TBATCH = 8
LAT_DEV = 8


POLY_COEFFS = (1.0, -0.6, 0.15, -0.03)


def with_halo(shard, sides, width):
    for axis, dim in sides:
        devices, length = (lax.axis_size(axis), shard.shape[dim])
        up = [(i, (i + 1) % devices) for i in range(devices - 1)]
        down = [(j, i) for i, j in up]
        last = lax.slice_in_dim(shard, length - width, length, axis=dim)
        leading = lax.slice_in_dim(shard, 0, width, axis=dim)
        before = lax.ppermute(last, axis, up)
        after = lax.ppermute(leading, axis, down)
        shard = jnp.concatenate([before, shard, after], axis=dim)
    return shard


def complex_times(left_real, left_imag, right_real, right_imag):
    level = lax.Precision.HIGH
    real_part = jnp.dot(
        left_real, right_real, precision=level, preferred_element_type=jnp.float32
    ) - jnp.dot(left_imag, right_imag, precision=level, preferred_element_type=jnp.float32)
    imag_part = jnp.dot(
        left_real, right_imag, precision=level, preferred_element_type=jnp.float32
    ) + jnp.dot(left_imag, right_real, precision=level, preferred_element_type=jnp.float32)
    return (real_part, imag_part)


def tile_pass(flat_echo, weights, tile_goal, tile_start, live_total, tiles_out):
    tile_size = weights.shape[-1]
    col_count = flat_echo.shape[-1]
    slot_count = weights.shape[0]
    lane_ids = jnp.arange(TBATCH, dtype=jnp.int32)
    target_ids = jnp.arange(tiles_out, dtype=jnp.int32)
    zero_index = jnp.zeros((), jnp.int32)

    def cut_rows(offset_id):
        return lax.dynamic_slice(flat_echo, (offset_id, zero_index), (tile_size, col_count))

    def one_turn(turn_index, totals):
        where_at = turn_index * TBATCH + lane_ids
        live_lane = where_at < live_total
        chosen = jnp.minimum(where_at, slot_count - 1)
        picked = weights[chosen]
        samples = jax.vmap(cut_rows)(tile_start[chosen])
        product = jnp.einsum("krs,ksc->krc", picked, samples, preferred_element_type=jnp.float32)
        placing = ((tile_goal[chosen][:, None] == target_ids[None, :]) & live_lane[:, None]).astype(
            jnp.float32
        )
        return totals + jnp.einsum(
            "kt,krc->trc", placing, product, precision=lax.Precision.HIGHEST
        )

    start_totals = jnp.zeros((tiles_out, tile_size, col_count), jnp.float32)
    turn_count = (live_total + TBATCH - 1) // TBATCH
    return lax.fori_loop(0, turn_count, one_turn, start_totals)


def shards(echo_data, tile_weights, tile_target, tile_offset, tile_count, grid_map, psf_kernel):
    row_count = echo_data.shape[2]
    half_frames = echo_data.shape[4]
    tile_size = tile_weights.shape[-1]
    slot_count = tile_weights.shape[2]
    voxels = grid_map.shape[1]
    tiles_out = voxels // tile_size
    flat_echo = echo_data.reshape(row_count, 2 * half_frames)
    weights = tile_weights.reshape(slot_count, tile_size, tile_size)
    tile_sums = tile_pass(
        flat_echo,
        weights,
        tile_target.reshape(-1),
        tile_offset.reshape(-1),
        tile_count[0, 0],
        tiles_out,
    )
    arranged = jnp.take(tile_sums.reshape(voxels, 2, half_frames), grid_map[0], axis=0)
    arranged = arranged.reshape(LAT_DEV, voxels // LAT_DEV, 2, half_frames)
    beamformed = lax.psum_scatter(arranged, "chan", scatter_dimension=1, tiled=True).astype(
        jnp.bfloat16
    )
    lat_count = beamformed.shape[0]
    depth_count = beamformed.shape[1]
    cell_count = lat_count * depth_count
    own_frames = beamformed.reshape(cell_count, 2, half_frames)
    all_frames = lax.all_gather(own_frames, "frm", axis=2, tiled=True)
    frames = all_frames.shape[2]
    own_flat = own_frames.reshape(cell_count, 2 * half_frames)
    all_flat = all_frames.reshape(cell_count, 2 * frames)
    gram_block = lax.dot_general(
        own_flat, all_flat, (((0,), (0,)), ((), ())), preferred_element_type=jnp.float32
    )
    gram_real = gram_block[:half_frames, :frames] + gram_block[half_frames:, frames:]
    gram_imag = gram_block[:half_frames, frames:] - gram_block[half_frames:, :frames]
    frame_start = lax.axis_index("frm") * half_frames
    echo_real = all_frames[:, 0, :].astype(jnp.float32)
    echo_imag = all_frames[:, 1, :].astype(jnp.float32)
    energy = jnp.sum(echo_real * echo_real + echo_imag * echo_imag)
    gram_real, gram_imag, trace_value = lax.psum((gram_real, gram_imag, energy), ("vox", "chan"))
    factor = frames / trace_value
    norm_real = factor * gram_real
    norm_imag = factor * gram_imag
    full_real, full_imag = (
        lax.all_gather(norm_real, "frm", axis=0, tiled=True),
        lax.all_gather(norm_imag, "frm", axis=0, tiled=True),
    )
    identity = jnp.eye(frames, dtype=jnp.float32)
    poly_real = POLY_COEFFS[3] * full_real + POLY_COEFFS[2] * identity
    poly_imag = POLY_COEFFS[3] * full_imag
    poly_real, poly_imag = complex_times(poly_real, poly_imag, full_real, full_imag)
    poly_real = poly_real + POLY_COEFFS[1] * identity
    cols_real = lax.dynamic_slice_in_dim(full_real, frame_start, half_frames, 1)
    cols_imag = lax.dynamic_slice_in_dim(full_imag, frame_start, half_frames, 1)
    filter_real, filter_imag = complex_times(poly_real, poly_imag, cols_real, cols_imag)
    filter_real = filter_real + POLY_COEFFS[0] * lax.dynamic_slice_in_dim(
        identity, frame_start, half_frames, 1
    )
    out_real, out_imag = complex_times(echo_real, echo_imag, filter_real, filter_imag)
    envelope = jnp.sqrt(out_real * out_real + out_imag * out_imag + 1e-06)
    envelope = envelope.reshape(lat_count, depth_count, half_frames)
    padded = with_halo(envelope, (("vox", 0), ("chan", 1)), 2)
    psf_image = jnp.zeros_like(envelope)
    for shift_a in range(5):
        for shift_b in range(5):
            psf_image = (
                psf_image
                + psf_kernel[shift_a, shift_b]
                * padded[shift_a : shift_a + lat_count, shift_b : shift_b + depth_count]
            )
    return psf_image


def split(value):
    high = value.astype(jnp.bfloat16)
    return high, (value - high.astype(jnp.float32)).astype(jnp.bfloat16)


def beam_kernel(goal_ref, start_ref, live_ref, weights_ref, echo_ref, map_ref, out_ref, small_ref, operator, high_ref, low_ref):
    blocks, voxels, tile = operator.shape
    operator[...] = jnp.zeros_like(operator)
    lane = lax.broadcasted_iota(jnp.int32, (tile, tile), 1)

    slots = weights_ref.shape[0]
    live = live_ref[0]

    def place(turn, carry):
        ready = []
        for index in range(GROUP):
            slot = turn * GROUP + index
            kept = jnp.minimum(slot, slots - 1)
            first = start_ref[kept]
            block = first // tile
            shift = first - block * tile
            rows = pl.ds(pl.multiple_of(goal_ref[kept] * tile, tile), tile)
            turned = pltpu.roll(weights_ref[kept].astype(jnp.float32), shift, 1)
            limit = jnp.where(slot < live, shift, tile)
            least = jnp.where(slot < live, 0, tile)
            ready.append((block, rows, jnp.where(lane >= limit, turned, 0.0), turned, shift, least))
        for block, rows, high, turned, shift, least in ready:
            operator[block, rows, :] += high
            operator[block + 1, rows, :] += jnp.where((lane < shift) & (lane >= least), turned, 0.0)
        return carry

    lax.fori_loop(0, (live + GROUP - 1) // GROUP, place, 0)
    picks = lax.broadcasted_iota(jnp.int32, (voxels, voxels), 0) == map_ref[...]
    picks = picks.astype(jnp.float32).T.astype(jnp.bfloat16)
    for block in range(blocks - 1):
        high, low = split(operator[block])
        columns = slice(block * tile, (block + 1) * tile)
        for part, target in ((high, high_ref), (low, low_ref)):
            moved = jnp.dot(picks, part, preferred_element_type=jnp.float32)
            target[:, columns] = moved.astype(jnp.bfloat16)
    sums = jnp.dot(high_ref[...], echo_ref[...], preferred_element_type=jnp.float32)
    sums += jnp.dot(low_ref[...], echo_ref[...], preferred_element_type=jnp.float32)
    halves, cells, _ = out_ref.shape
    width = cells // LAT_DEV
    for lat in range(LAT_DEV):
        for half in range(halves):
            source = (lat * halves + half) * width
            chosen = sums[source : source + width]
            out_ref[half, lat * width : (lat + 1) * width, :] = chosen
            small_ref[half, lat * width : (lat + 1) * width, :] = chosen.astype(small_ref.dtype)


def gather_kernel(
    count, part_ref, small_ref, out_ref, arrived, swap_send, swap_recv, own_recv, mate_recv, up_send, down_send, mate_send
):
    vox, chan, frm = lax.axis_index("vox"), lax.axis_index("chan"), lax.axis_index("frm")
    beside, mate = {"chan": 1 - chan}, {"frm": 1 - frm}
    above, below = {"vox": vox + 1}, {"vox": vox - 1}
    can_up, can_down = vox + 1 < count, vox > 0
    pieces = swap_send.shape[0]
    height = part_ref.shape[1] // pieces
    barrier = pltpu.get_barrier_semaphore()

    def greet(target):
        pl.semaphore_signal(barrier, inc=1, device_id=target, device_id_type=MESH)

    greet(beside)
    greet(mate)
    pl.when(can_up)(lambda: greet(above))
    pl.when(can_down)(lambda: greet(below))
    pl.semaphore_wait(barrier, 4 - jnp.where(can_up, 0, 1) - jnp.where(can_down, 0, 1))

    def remote(source, target, sent, received, device):
        return pltpu.make_async_remote_copy(
            src_ref=source, dst_ref=target, send_sem=sent, recv_sem=received, device_id=device, device_id_type=MESH
        )

    def rows(piece):
        return pl.ds(piece * height, height)

    def item(block, piece, sent, device):
        place = out_ref.at[block, frm, :, rows(piece)]
        return remote(place, place, sent, own_recv.at[block, piece], device)

    def to_mate(block, piece, owner=None):
        place = out_ref.at[block, frm if owner is None else owner, :, rows(piece)]
        return remote(place, place, mate_send.at[block, piece], mate_recv.at[block, piece], mate)

    def go_up(block, piece):
        return item(block, piece, up_send.at[block, piece], above)

    def go_down(block, piece):
        return item(block, piece, down_send.at[block, piece], below)

    def swap(piece):
        return remote(
            small_ref.at[:, rows(piece)], arrived.at[:, rows(piece)], swap_send.at[piece], swap_recv.at[piece], beside
        )

    def relay(step, piece):
        @pl.when(vox >= step)
        def _():
            item(vox - step, piece, up_send.at[0, piece], above).wait_recv()
            pl.when(can_up)(lambda: go_up(vox - step, piece).start())
            to_mate(vox - step, piece).start()

        @pl.when(vox + step < count)
        def _():
            item(vox + step, piece, down_send.at[0, piece], below).wait_recv()
            pl.when(can_down)(lambda: go_down(vox + step, piece).start())
            to_mate(vox + step, piece).start()

    for piece in range(pieces):
        swap(piece).start()
    for wave in range(pieces + count - 1):
        if wave < pieces:
            swap(wave).wait_recv()
            mine = part_ref[:, rows(wave)] + arrived[:, rows(wave)].astype(jnp.float32)
            out_ref[vox, frm, :, rows(wave)] = mine.astype(out_ref.dtype)
            pl.when(can_up)(lambda: go_up(vox, wave).start())
            pl.when(can_down)(lambda: go_down(vox, wave).start())
            to_mate(vox, wave).start()
        for step in range(1, count):
            piece = wave - step
            if 0 <= piece < pieces:
                relay(step, piece)

    for piece in range(pieces):
        swap(piece).wait_send()
        for block in range(count):
            to_mate(block, piece).wait_send()
            to_mate(block, piece, 1 - frm).wait_recv()
            pl.when(can_up & (vox >= block))(lambda: go_up(block, piece).wait_send())
            pl.when(can_down & (vox <= block))(lambda: go_down(block, piece).wait_send())


def filter_kernel(count, beams_ref, psf_ref, out_ref, high_ref, low_ref, padded):
    vox, chan, frm = lax.axis_index("vox"), lax.axis_index("chan"), lax.axis_index("frm")
    lat, depth, half = out_ref.shape
    cells = lat * depth
    pair = 2 * half
    total = count * 2 * cells
    left = beams_ref[:, 0].reshape(total, pair)
    right = beams_ref[:, 1].reshape(total, pair)

    def gram(first, second):
        block = lax.dot_general(first, second, (((0,), (0,)), ((), ())), preferred_element_type=jnp.float32)
        real = block[:half, :half] + block[half:, half:]
        imag = block[:half, half:] - block[half:, :half]
        return real, imag

    grams = {(0, 0): gram(left, left), (0, 1): gram(left, right), (1, 1): gram(right, right)}
    grams[1, 0] = (grams[0, 1][0].T, -grams[0, 1][1].T)
    eye = lax.broadcasted_iota(jnp.int32, (half, half), 0) == lax.broadcasted_iota(jnp.int32, (half, half), 1)
    diagonal = jnp.where(eye, grams[0, 0][0] + grams[1, 1][0], 0.0)
    trace = jnp.sum(jnp.sum(diagonal, axis=0, keepdims=True), axis=1, keepdims=True)
    factor = (2 * half) / trace
    for (row, column), (real, imag) in grams.items():
        real_parts, imag_parts = split(factor * real), split(factor * imag)
        for target, real_part, imag_part in zip((high_ref, low_ref), real_parts, imag_parts):
            top, side = row * pair, column * pair
            target[top : top + half, side : side + half] = real_part
            target[top : top + half, side + half : side + pair] = imag_part
            target[top + half : top + pair, side : side + half] = -imag_part
            target[top + half : top + pair, side + half : side + pair] = real_part

    before, after = jnp.maximum(vox - 1, 0), jnp.minimum(vox + 1, count - 1)
    edge = 2 * depth

    def both(block, side, rows):
        return jnp.concatenate([beams_ref[block, 0, side, rows], beams_ref[block, 1, side, rows]], axis=1)

    other = 1 - chan
    near = jnp.concatenate(
        [
            both(before, other, slice(cells - edge, cells)),
            both(vox, other, slice(0, cells)),
            both(after, other, slice(0, edge)),
        ],
        axis=0,
    )
    tall = lat + 4
    slots = -(-2 * tall // 16) * 16
    picked = lax.broadcasted_iota(jnp.int32, (slots, tall * depth), 0)
    source = lax.broadcasted_iota(jnp.int32, (slots, tall * depth), 1)
    wanted = (picked // 2) * depth + picked % 2 + jnp.where(chan == 0, 0, depth - 2)
    picks = ((source == wanted) & (picked < 2 * tall)).astype(jnp.float32).astype(jnp.bfloat16)
    near = jnp.dot(picks, near, preferred_element_type=jnp.float32).astype(jnp.bfloat16)
    beams = jnp.concatenate(
        [
            both(before, chan, slice(cells - edge, cells)),
            both(vox, chan, slice(0, cells)),
            both(after, chan, slice(0, edge)),
            near,
        ],
        axis=0,
    )

    def times(left, right_ref, columns):
        return jnp.dot(left, right_ref[:, columns], preferred_element_type=jnp.float32)

    echo = beams.astype(jnp.float32)
    whole = slice(0, 2 * pair)
    term = POLY_COEFFS[3] * times(beams, high_ref, whole) + POLY_COEFFS[2] * echo
    term = times(term.astype(jnp.bfloat16), high_ref, whole) + POLY_COEFFS[1] * echo
    own = pl.ds(pl.multiple_of(frm * pair, pair), pair)
    echo = jnp.where(frm == 0, echo[:, :pair], echo[:, pair:])
    high, low = split(term)
    term = times(high, high_ref, own) + times(high, low_ref, own) + times(low, high_ref, own) + POLY_COEFFS[0] * echo
    envelope = jnp.sqrt(term[:, :half] * term[:, :half] + term[:, half:] * term[:, half:] + 1e-06)

    padded[...] = jnp.zeros_like(padded)
    has_before, has_after = jnp.where(vox > 0, 1.0, 0.0), jnp.where(vox + 1 < count, 1.0, 0.0)
    right_side, left_side = jnp.where(chan == 0, 1.0, 0.0), jnp.where(chan == 0, 0.0, 1.0)
    for line in range(tall):
        scale = has_before if line < 2 else has_after if line >= lat + 2 else None
        middle = envelope[line * depth : (line + 1) * depth]
        start = tall * depth + 2 * line
        rim = envelope[start : start + 2]
        if scale is not None:
            middle, rim = middle * scale, rim * scale
        padded[line, 8 : 8 + depth, :] = middle
        padded[line, 6:8, :] = rim * left_side
        padded[line, 8 + depth : 10 + depth, :] = rim * right_side
    result = jnp.zeros((lat, depth, half), jnp.float32)
    for shift_b in range(5):
        for shift_a in range(5):
            result += psf_ref[shift_a, shift_b] * padded[shift_a : shift_a + lat, 6 + shift_b : 6 + shift_b + depth]
    out_ref[...] = result


def kernel_shards(count, echo_data, tile_weights, tile_target, tile_offset, tile_count, grid_map, psf_kernel):
    rows, half = echo_data.shape[2], echo_data.shape[4]
    slots, tile = tile_weights.shape[2], tile_weights.shape[4]
    voxels = grid_map.shape[1]
    cells, pair = voxels // 2, 2 * half
    depth = cells // LAT_DEV
    vmem, smem = pl.BlockSpec(memory_space=pltpu.VMEM), pl.BlockSpec(memory_space=pltpu.SMEM)
    parts, small = pl.pallas_call(
        beam_kernel,
        name="beam",
        out_shape=[
            jax.ShapeDtypeStruct((2, cells, pair), jnp.float32),
            jax.ShapeDtypeStruct((2, cells, pair), jnp.bfloat16),
        ],
        in_specs=[smem, smem, smem, vmem, vmem, vmem],
        out_specs=[vmem, vmem],
        scratch_shapes=[
            pltpu.VMEM((rows // tile + 1, voxels, tile), jnp.float32),
            pltpu.VMEM((voxels, rows), jnp.bfloat16),
            pltpu.VMEM((voxels, rows), jnp.bfloat16),
        ],
    )(
        tile_target.reshape(-1),
        tile_offset.reshape(-1),
        tile_count.reshape(-1),
        tile_weights.reshape(slots, tile, tile),
        echo_data.reshape(rows, pair),
        grid_map,
    )
    pieces = PIECES
    each = (count, pieces)
    dma = pltpu.SemaphoreType.DMA
    beams = pl.pallas_call(
        functools.partial(gather_kernel, count),
        name="gather",
        out_shape=jax.ShapeDtypeStruct((count, 2, 2, cells, pair), jnp.bfloat16),
        in_specs=[vmem, vmem],
        out_specs=vmem,
        scratch_shapes=[pltpu.VMEM((2, cells, pair), jnp.bfloat16)] + [dma((pieces,))] * 2 + [dma(each)] * 5,
        compiler_params=pltpu.CompilerParams(collective_id=0, has_side_effects=True),
    )(parts, small)
    return pl.pallas_call(
        functools.partial(filter_kernel, count),
        name="filter",
        out_shape=jax.ShapeDtypeStruct((LAT_DEV, depth, half), jnp.float32),
        in_specs=[vmem, smem],
        out_specs=vmem,
        scratch_shapes=[
            pltpu.VMEM((2 * pair, 2 * pair), jnp.bfloat16),
            pltpu.VMEM((2 * pair, 2 * pair), jnp.bfloat16),
            pltpu.VMEM((LAT_DEV + 4, depth + 16, half), jnp.float32),
        ],
    )(beams, psf_kernel)


def solution(mesh):
    in_specs = (
        P(("groups", "vox"), "chan", None, None, "frm"),
        P("vox", "chan", None, None, None),
        P("vox", "chan", None),
        P("vox", "chan", None),
        P("vox", "chan"),
        P("vox", None),
        P(),
    )
    out_specs = P(("groups", "vox"), "chan", "frm")
    body = shards
    if mesh.shape["chan"] == 2 and mesh.shape["frm"] == 2:
        body = functools.partial(kernel_shards, mesh.shape["vox"])
    return jax.shard_map(body, mesh=mesh, in_specs=in_specs, out_specs=out_specs, check_vma=False)
```

```python
import functools

import jax
import jax.numpy as jnp
from jax import lax
from jax.experimental import pallas as pl
from jax.experimental.pallas import tpu as pltpu
from jax.sharding import PartitionSpec as P

MESH = pl.DeviceIdType.MESH
PIECES = 4
GROUP = 8

TBATCH = 8
LAT_DEV = 8


POLY_COEFFS = (1.0, -0.6, 0.15, -0.03)


def with_halo(shard, sides, width):
    for axis, dim in sides:
        devices, length = (lax.axis_size(axis), shard.shape[dim])
        up = [(i, (i + 1) % devices) for i in range(devices - 1)]
        down = [(j, i) for i, j in up]
        last = lax.slice_in_dim(shard, length - width, length, axis=dim)
        leading = lax.slice_in_dim(shard, 0, width, axis=dim)
        before = lax.ppermute(last, axis, up)
        after = lax.ppermute(leading, axis, down)
        shard = jnp.concatenate([before, shard, after], axis=dim)
    return shard


def complex_times(left_real, left_imag, right_real, right_imag):
    level = lax.Precision.HIGH
    real_part = jnp.dot(
        left_real, right_real, precision=level, preferred_element_type=jnp.float32
    ) - jnp.dot(left_imag, right_imag, precision=level, preferred_element_type=jnp.float32)
    imag_part = jnp.dot(
        left_real, right_imag, precision=level, preferred_element_type=jnp.float32
    ) + jnp.dot(left_imag, right_real, precision=level, preferred_element_type=jnp.float32)
    return (real_part, imag_part)


def tile_pass(flat_echo, weights, tile_goal, tile_start, live_total, tiles_out):
    tile_size = weights.shape[-1]
    col_count = flat_echo.shape[-1]
    slot_count = weights.shape[0]
    lane_ids = jnp.arange(TBATCH, dtype=jnp.int32)
    target_ids = jnp.arange(tiles_out, dtype=jnp.int32)
    zero_index = jnp.zeros((), jnp.int32)

    def cut_rows(offset_id):
        return lax.dynamic_slice(flat_echo, (offset_id, zero_index), (tile_size, col_count))

    def one_turn(turn_index, totals):
        where_at = turn_index * TBATCH + lane_ids
        live_lane = where_at < live_total
        chosen = jnp.minimum(where_at, slot_count - 1)
        picked = weights[chosen]
        samples = jax.vmap(cut_rows)(tile_start[chosen])
        product = jnp.einsum("krs,ksc->krc", picked, samples, preferred_element_type=jnp.float32)
        placing = ((tile_goal[chosen][:, None] == target_ids[None, :]) & live_lane[:, None]).astype(
            jnp.float32
        )
        return totals + jnp.einsum(
            "kt,krc->trc", placing, product, precision=lax.Precision.HIGHEST
        )

    start_totals = jnp.zeros((tiles_out, tile_size, col_count), jnp.float32)
    turn_count = (live_total + TBATCH - 1) // TBATCH
    return lax.fori_loop(0, turn_count, one_turn, start_totals)


def shards(echo_data, tile_weights, tile_target, tile_offset, tile_count, grid_map, psf_kernel):
    row_count = echo_data.shape[2]
    half_frames = echo_data.shape[4]
    tile_size = tile_weights.shape[-1]
    slot_count = tile_weights.shape[2]
    voxels = grid_map.shape[1]
    tiles_out = voxels // tile_size
    flat_echo = echo_data.reshape(row_count, 2 * half_frames)
    weights = tile_weights.reshape(slot_count, tile_size, tile_size)
    tile_sums = tile_pass(
        flat_echo,
        weights,
        tile_target.reshape(-1),
        tile_offset.reshape(-1),
        tile_count[0, 0],
        tiles_out,
    )
    arranged = jnp.take(tile_sums.reshape(voxels, 2, half_frames), grid_map[0], axis=0)
    arranged = arranged.reshape(LAT_DEV, voxels // LAT_DEV, 2, half_frames)
    beamformed = lax.psum_scatter(arranged, "chan", scatter_dimension=1, tiled=True).astype(
        jnp.bfloat16
    )
    lat_count = beamformed.shape[0]
    depth_count = beamformed.shape[1]
    cell_count = lat_count * depth_count
    own_frames = beamformed.reshape(cell_count, 2, half_frames)
    all_frames = lax.all_gather(own_frames, "frm", axis=2, tiled=True)
    frames = all_frames.shape[2]
    own_flat = own_frames.reshape(cell_count, 2 * half_frames)
    all_flat = all_frames.reshape(cell_count, 2 * frames)
    gram_block = lax.dot_general(
        own_flat, all_flat, (((0,), (0,)), ((), ())), preferred_element_type=jnp.float32
    )
    gram_real = gram_block[:half_frames, :frames] + gram_block[half_frames:, frames:]
    gram_imag = gram_block[:half_frames, frames:] - gram_block[half_frames:, :frames]
    frame_start = lax.axis_index("frm") * half_frames
    echo_real = all_frames[:, 0, :].astype(jnp.float32)
    echo_imag = all_frames[:, 1, :].astype(jnp.float32)
    energy = jnp.sum(echo_real * echo_real + echo_imag * echo_imag)
    gram_real, gram_imag, trace_value = lax.psum((gram_real, gram_imag, energy), ("vox", "chan"))
    factor = frames / trace_value
    norm_real = factor * gram_real
    norm_imag = factor * gram_imag
    full_real, full_imag = (
        lax.all_gather(norm_real, "frm", axis=0, tiled=True),
        lax.all_gather(norm_imag, "frm", axis=0, tiled=True),
    )
    identity = jnp.eye(frames, dtype=jnp.float32)
    poly_real = POLY_COEFFS[3] * full_real + POLY_COEFFS[2] * identity
    poly_imag = POLY_COEFFS[3] * full_imag
    poly_real, poly_imag = complex_times(poly_real, poly_imag, full_real, full_imag)
    poly_real = poly_real + POLY_COEFFS[1] * identity
    cols_real = lax.dynamic_slice_in_dim(full_real, frame_start, half_frames, 1)
    cols_imag = lax.dynamic_slice_in_dim(full_imag, frame_start, half_frames, 1)
    filter_real, filter_imag = complex_times(poly_real, poly_imag, cols_real, cols_imag)
    filter_real = filter_real + POLY_COEFFS[0] * lax.dynamic_slice_in_dim(
        identity, frame_start, half_frames, 1
    )
    out_real, out_imag = complex_times(echo_real, echo_imag, filter_real, filter_imag)
    envelope = jnp.sqrt(out_real * out_real + out_imag * out_imag + 1e-06)
    envelope = envelope.reshape(lat_count, depth_count, half_frames)
    padded = with_halo(envelope, (("vox", 0), ("chan", 1)), 2)
    psf_image = jnp.zeros_like(envelope)
    for shift_a in range(5):
        for shift_b in range(5):
            psf_image = (
                psf_image
                + psf_kernel[shift_a, shift_b]
                * padded[shift_a : shift_a + lat_count, shift_b : shift_b + depth_count]
            )
    return psf_image


def split(value):
    high = value.astype(jnp.bfloat16)
    return high, (value - high.astype(jnp.float32)).astype(jnp.bfloat16)


def beam_kernel(goal_ref, start_ref, live_ref, weights_hbm, echo_hbm, map_ref, out_ref, small_ref, operator, high_ref, low_ref, weights_ref, echo_ref, weights_sem, echo_sem):
    blocks, voxels, tile = operator.shape
    slots = weights_ref.shape[0]
    live = live_ref[0]
    turns = (live + GROUP - 1) // GROUP

    def fetch(turn):
        chunk = pl.ds(turn * GROUP, GROUP)
        return pltpu.make_async_copy(weights_hbm.at[chunk], weights_ref.at[chunk], weights_sem.at[turn])

    def begin(turn, carry):
        fetch(turn).start()
        return carry

    lax.fori_loop(0, turns, begin, 0)
    echo_copy = pltpu.make_async_copy(echo_hbm, echo_ref, echo_sem.at[0])
    echo_copy.start()
    operator[...] = jnp.zeros_like(operator)
    lane = lax.broadcasted_iota(jnp.int32, (tile, tile), 1)


    def place(turn, carry):
        fetch(turn).wait()
        ready = []
        for index in range(GROUP):
            slot = turn * GROUP + index
            kept = jnp.minimum(slot, slots - 1)
            first = start_ref[kept]
            block = first // tile
            shift = first - block * tile
            rows = pl.ds(pl.multiple_of(goal_ref[kept] * tile, tile), tile)
            turned = pltpu.roll(weights_ref[kept].astype(jnp.float32), shift, 1)
            limit = jnp.where(slot < live, shift, tile)
            least = jnp.where(slot < live, 0, tile)
            ready.append((block, rows, jnp.where(lane >= limit, turned, 0.0), turned, shift, least))
        for block, rows, high, turned, shift, least in ready:
            operator[block, rows, :] += high
            operator[block + 1, rows, :] += jnp.where((lane < shift) & (lane >= least), turned, 0.0)
        return carry

    lax.fori_loop(0, turns, place, 0)
    picks = lax.broadcasted_iota(jnp.int32, (voxels, voxels), 0) == map_ref[...]
    picks = picks.astype(jnp.float32).T.astype(jnp.bfloat16)
    for block in range(blocks - 1):
        high, low = split(operator[block])
        columns = slice(block * tile, (block + 1) * tile)
        for part, target in ((high, high_ref), (low, low_ref)):
            moved = jnp.dot(picks, part, preferred_element_type=jnp.float32)
            target[:, columns] = moved.astype(jnp.bfloat16)
    echo_copy.wait()
    sums = jnp.dot(high_ref[...], echo_ref[...], preferred_element_type=jnp.float32)
    sums += jnp.dot(low_ref[...], echo_ref[...], preferred_element_type=jnp.float32)
    halves, cells, _ = out_ref.shape
    width = cells // LAT_DEV
    for lat in range(LAT_DEV):
        for half in range(halves):
            source = (lat * halves + half) * width
            chosen = sums[source : source + width]
            out_ref[half, lat * width : (lat + 1) * width, :] = chosen
            small_ref[half, lat * width : (lat + 1) * width, :] = chosen.astype(small_ref.dtype)


def gather_kernel(
    count, part_ref, small_ref, out_ref, arrived, swap_send, swap_recv, own_recv, mate_recv, up_send, down_send, mate_send
):
    vox, chan, frm = lax.axis_index("vox"), lax.axis_index("chan"), lax.axis_index("frm")
    beside, mate = {"chan": 1 - chan}, {"frm": 1 - frm}
    above, below = {"vox": vox + 1}, {"vox": vox - 1}
    can_up, can_down = vox + 1 < count, vox > 0
    pieces = swap_send.shape[0]
    height = part_ref.shape[1] // pieces
    barrier = pltpu.get_barrier_semaphore()

    def greet(target):
        pl.semaphore_signal(barrier, inc=1, device_id=target, device_id_type=MESH)

    greet(beside)
    greet(mate)
    pl.when(can_up)(lambda: greet(above))
    pl.when(can_down)(lambda: greet(below))
    pl.semaphore_wait(barrier, 4 - jnp.where(can_up, 0, 1) - jnp.where(can_down, 0, 1))

    def remote(source, target, sent, received, device):
        return pltpu.make_async_remote_copy(
            src_ref=source, dst_ref=target, send_sem=sent, recv_sem=received, device_id=device, device_id_type=MESH
        )

    def rows(piece):
        return pl.ds(piece * height, height)

    def item(block, piece, sent, device):
        place = out_ref.at[block, frm, :, rows(piece)]
        return remote(place, place, sent, own_recv.at[block, piece], device)

    def to_mate(block, piece, owner=None):
        place = out_ref.at[block, frm if owner is None else owner, :, rows(piece)]
        return remote(place, place, mate_send.at[block, piece], mate_recv.at[block, piece], mate)

    def go_up(block, piece):
        return item(block, piece, up_send.at[block, piece], above)

    def go_down(block, piece):
        return item(block, piece, down_send.at[block, piece], below)

    def swap(piece):
        return remote(
            small_ref.at[:, rows(piece)], arrived.at[:, rows(piece)], swap_send.at[piece], swap_recv.at[piece], beside
        )

    def relay(step, piece):
        @pl.when(vox >= step)
        def _():
            item(vox - step, piece, up_send.at[0, piece], above).wait_recv()
            pl.when(can_up)(lambda: go_up(vox - step, piece).start())
            to_mate(vox - step, piece).start()

        @pl.when(vox + step < count)
        def _():
            item(vox + step, piece, down_send.at[0, piece], below).wait_recv()
            pl.when(can_down)(lambda: go_down(vox + step, piece).start())
            to_mate(vox + step, piece).start()

    for piece in range(pieces):
        swap(piece).start()
    for wave in range(pieces + count - 1):
        if wave < pieces:
            swap(wave).wait_recv()
            mine = part_ref[:, rows(wave)] + arrived[:, rows(wave)].astype(jnp.float32)
            out_ref[vox, frm, :, rows(wave)] = mine.astype(out_ref.dtype)
            pl.when(can_up)(lambda: go_up(vox, wave).start())
            pl.when(can_down)(lambda: go_down(vox, wave).start())
            to_mate(vox, wave).start()
        for step in range(1, count):
            piece = wave - step
            if 0 <= piece < pieces:
                relay(step, piece)

    for piece in range(pieces):
        swap(piece).wait_send()
        for block in range(count):
            to_mate(block, piece).wait_send()
            to_mate(block, piece, 1 - frm).wait_recv()
            pl.when(can_up & (vox >= block))(lambda: go_up(block, piece).wait_send())
            pl.when(can_down & (vox <= block))(lambda: go_down(block, piece).wait_send())


def filter_kernel(count, beams_ref, psf_ref, out_ref, high_ref, low_ref, padded):
    vox, chan, frm = lax.axis_index("vox"), lax.axis_index("chan"), lax.axis_index("frm")
    lat, depth, half = out_ref.shape
    cells = lat * depth
    pair = 2 * half
    total = count * 2 * cells
    left = beams_ref[:, 0].reshape(total, pair)
    right = beams_ref[:, 1].reshape(total, pair)

    def gram(first, second):
        block = lax.dot_general(first, second, (((0,), (0,)), ((), ())), preferred_element_type=jnp.float32)
        real = block[:half, :half] + block[half:, half:]
        imag = block[:half, half:] - block[half:, :half]
        return real, imag

    grams = {(0, 0): gram(left, left), (0, 1): gram(left, right), (1, 1): gram(right, right)}
    grams[1, 0] = (grams[0, 1][0].T, -grams[0, 1][1].T)
    eye = lax.broadcasted_iota(jnp.int32, (half, half), 0) == lax.broadcasted_iota(jnp.int32, (half, half), 1)
    diagonal = jnp.where(eye, grams[0, 0][0] + grams[1, 1][0], 0.0)
    trace = jnp.sum(jnp.sum(diagonal, axis=0, keepdims=True), axis=1, keepdims=True)
    factor = (2 * half) / trace
    for (row, column), (real, imag) in grams.items():
        real_parts, imag_parts = split(factor * real), split(factor * imag)
        for target, real_part, imag_part in zip((high_ref, low_ref), real_parts, imag_parts):
            top, side = row * pair, column * pair
            target[top : top + half, side : side + half] = real_part
            target[top : top + half, side + half : side + pair] = imag_part
            target[top + half : top + pair, side : side + half] = -imag_part
            target[top + half : top + pair, side + half : side + pair] = real_part

    before, after = jnp.maximum(vox - 1, 0), jnp.minimum(vox + 1, count - 1)
    edge = 2 * depth

    def both(block, side, rows):
        return jnp.concatenate([beams_ref[block, 0, side, rows], beams_ref[block, 1, side, rows]], axis=1)

    other = 1 - chan
    near = jnp.concatenate(
        [
            both(before, other, slice(cells - edge, cells)),
            both(vox, other, slice(0, cells)),
            both(after, other, slice(0, edge)),
        ],
        axis=0,
    )
    tall = lat + 4
    slots = -(-2 * tall // 16) * 16
    picked = lax.broadcasted_iota(jnp.int32, (slots, tall * depth), 0)
    source = lax.broadcasted_iota(jnp.int32, (slots, tall * depth), 1)
    wanted = (picked // 2) * depth + picked % 2 + jnp.where(chan == 0, 0, depth - 2)
    picks = ((source == wanted) & (picked < 2 * tall)).astype(jnp.float32).astype(jnp.bfloat16)
    near = jnp.dot(picks, near, preferred_element_type=jnp.float32).astype(jnp.bfloat16)
    beams = jnp.concatenate(
        [
            both(before, chan, slice(cells - edge, cells)),
            both(vox, chan, slice(0, cells)),
            both(after, chan, slice(0, edge)),
            near,
        ],
        axis=0,
    )

    def times(left, right_ref, columns):
        return jnp.dot(left, right_ref[:, columns], preferred_element_type=jnp.float32)

    echo = beams.astype(jnp.float32)
    whole = slice(0, 2 * pair)
    term = POLY_COEFFS[3] * times(beams, high_ref, whole) + POLY_COEFFS[2] * echo
    term = times(term.astype(jnp.bfloat16), high_ref, whole) + POLY_COEFFS[1] * echo
    own = pl.ds(pl.multiple_of(frm * pair, pair), pair)
    echo = jnp.where(frm == 0, echo[:, :pair], echo[:, pair:])
    high, low = split(term)
    term = times(high, high_ref, own) + times(high, low_ref, own) + times(low, high_ref, own) + POLY_COEFFS[0] * echo
    envelope = jnp.sqrt(term[:, :half] * term[:, :half] + term[:, half:] * term[:, half:] + 1e-06)

    padded[...] = jnp.zeros_like(padded)
    has_before, has_after = jnp.where(vox > 0, 1.0, 0.0), jnp.where(vox + 1 < count, 1.0, 0.0)
    right_side, left_side = jnp.where(chan == 0, 1.0, 0.0), jnp.where(chan == 0, 0.0, 1.0)
    for line in range(tall):
        scale = has_before if line < 2 else has_after if line >= lat + 2 else None
        middle = envelope[line * depth : (line + 1) * depth]
        start = tall * depth + 2 * line
        rim = envelope[start : start + 2]
        if scale is not None:
            middle, rim = middle * scale, rim * scale
        padded[line, 8 : 8 + depth, :] = middle
        padded[line, 6:8, :] = rim * left_side
        padded[line, 8 + depth : 10 + depth, :] = rim * right_side
    result = jnp.zeros((lat, depth, half), jnp.float32)
    for shift_b in range(5):
        for shift_a in range(5):
            result += psf_ref[shift_a, shift_b] * padded[shift_a : shift_a + lat, 6 + shift_b : 6 + shift_b + depth]
    out_ref[...] = result


def kernel_shards(count, echo_data, tile_weights, tile_target, tile_offset, tile_count, grid_map, psf_kernel):
    rows, half = echo_data.shape[2], echo_data.shape[4]
    slots, tile = tile_weights.shape[2], tile_weights.shape[4]
    voxels = grid_map.shape[1]
    cells, pair = voxels // 2, 2 * half
    depth = cells // LAT_DEV
    vmem, smem = pl.BlockSpec(memory_space=pltpu.VMEM), pl.BlockSpec(memory_space=pltpu.SMEM)
    hbm = pl.BlockSpec(memory_space=pl.ANY)
    parts, small = pl.pallas_call(
        beam_kernel,
        name="beam",
        out_shape=[
            jax.ShapeDtypeStruct((2, cells, pair), jnp.float32),
            jax.ShapeDtypeStruct((2, cells, pair), jnp.bfloat16),
        ],
        in_specs=[smem, smem, smem, hbm, hbm, vmem],
        out_specs=[vmem, vmem],
        scratch_shapes=[
            pltpu.VMEM((rows // tile + 1, voxels, tile), jnp.float32),
            pltpu.VMEM((voxels, rows), jnp.bfloat16),
            pltpu.VMEM((voxels, rows), jnp.bfloat16),
            pltpu.VMEM((slots, tile, tile), jnp.bfloat16),
            pltpu.VMEM((rows, pair), jnp.bfloat16),
            pltpu.SemaphoreType.DMA((slots // GROUP,)),
            pltpu.SemaphoreType.DMA((1,)),
        ],
    )(
        tile_target.reshape(-1),
        tile_offset.reshape(-1),
        tile_count.reshape(-1),
        tile_weights.reshape(slots, tile, tile),
        echo_data.reshape(rows, pair),
        grid_map,
    )
    pieces = PIECES
    each = (count, pieces)
    dma = pltpu.SemaphoreType.DMA
    beams = pl.pallas_call(
        functools.partial(gather_kernel, count),
        name="gather",
        out_shape=jax.ShapeDtypeStruct((count, 2, 2, cells, pair), jnp.bfloat16),
        in_specs=[vmem, vmem],
        out_specs=vmem,
        scratch_shapes=[pltpu.VMEM((2, cells, pair), jnp.bfloat16)] + [dma((pieces,))] * 2 + [dma(each)] * 5,
        compiler_params=pltpu.CompilerParams(collective_id=0, has_side_effects=True),
    )(parts, small)
    return pl.pallas_call(
        functools.partial(filter_kernel, count),
        name="filter",
        out_shape=jax.ShapeDtypeStruct((LAT_DEV, depth, half), jnp.float32),
        in_specs=[vmem, smem],
        out_specs=vmem,
        scratch_shapes=[
            pltpu.VMEM((2 * pair, 2 * pair), jnp.bfloat16),
            pltpu.VMEM((2 * pair, 2 * pair), jnp.bfloat16),
            pltpu.VMEM((LAT_DEV + 4, depth + 16, half), jnp.float32),
        ],
    )(beams, psf_kernel)


def solution(mesh):
    in_specs = (
        P(("groups", "vox"), "chan", None, None, "frm"),
        P("vox", "chan", None, None, None),
        P("vox", "chan", None),
        P("vox", "chan", None),
        P("vox", "chan"),
        P("vox", None),
        P(),
    )
    out_specs = P(("groups", "vox"), "chan", "frm")
    body = shards
    if mesh.shape["chan"] == 2 and mesh.shape["frm"] == 2:
        body = functools.partial(kernel_shards, mesh.shape["vox"])
    return jax.shard_map(body, mesh=mesh, in_specs=in_specs, out_specs=out_specs, check_vma=False)
```
